256 devices in a mesh: sta: 64 (over y, z, core), tpl: 4 (over x).
Axes of the slice: x: 4, y: 4, z: 8, core: 2. Of those that a mesh axis runs over, the one named last changes fastest.
Arguments:
- records: bfloat16 [2048, 3, 1024], P(('sta', 'tpl')), may hold values from -180 to 180
- waveforms: bfloat16 [384, 64, 3, 256], P('tpl', 'sta'), may hold values from -54 to 54
- station_ids: int32 [384, 64], P('tpl', 'sta'), may hold values from 0 to 2047, as said below
- lag_steps: int32 [384, 64, 3], P('tpl', 'sta'), may hold values from 0 to 255
Outputs:
- network_stack: float32 [384, 512], P('tpl', 'sta')
The draws below stay inside these ranges and needn't reach their ends.
Inputs may be any that keep to these rules, and one draw needn't show every extreme that they name: `station_ids`: stations fall into aligned blocks of 32 (block = station // 32). Within each group of 96 consecutive templates, for every slot, at most 3 templates place that slot in the same block. Slot j of a template lies in block (b + j // 8) mod 64, where b is the block of its slot 0, so at most 24 templates of a group have some slot in one block, a number that some block reaches in every group. The stations of one template are distinct.
All inputs are finite; a program needn't handle non-finite values.
Results may differ from the reference program's by a relative error of at most 0.0003.
Values may be sent and summed in bfloat16 or wider, within the bound.
No kernel may reach another device: no remote copies, remote signals or barrier semaphores. Data moves between devices by JAX's collectives and lax.ppermute only.
A program may use at most 64 MiB of HBM per device.

```python
import math
import jax
import jax.numpy as jnp
from jax import lax

STA_DEV = 32
STATIONS = 2048
TEMPLATES = 384
TPL_GROUP = 96
TLEN = 256
MAXLAG = 256
WINDOW = 512
SLOTS = 64
CAP = 3
SAMPLES = 1024


def draw_records(key, part):
    key_noise, key_station, key_envelope = jax.random.split(key, 3)
    values = jax.random.truncated_normal(key_noise, -6.0, 6.0, (STATIONS, 3, SAMPLES), jnp.float32)
    station_gain = jnp.exp(jax.random.uniform(key_station, (STATIONS, 3, 1), jnp.float32, 0.0, math.log(3.0)))
    envelope = jnp.exp(jax.random.uniform(key_envelope, (STATIONS, 3, SAMPLES // 64, 1), jnp.float32, 0.0, math.log(10.0)))
    envelope = jnp.broadcast_to(envelope, (STATIONS, 3, SAMPLES // 64, 64)).reshape(STATIONS, 3, SAMPLES)
    return (values * station_gain * envelope).astype(jnp.bfloat16)


def draw_waveforms(key, part):
    key_noise, key_channel, key_piece = jax.random.split(key, 3)
    values = jax.random.truncated_normal(key_noise, -6.0, 6.0, (TEMPLATES, SLOTS, 3, TLEN), jnp.float32)
    channel_gain = jnp.exp(jax.random.uniform(key_channel, (TEMPLATES, SLOTS, 3, 1), jnp.float32, math.log(0.3), math.log(3.0)))
    piece_gain = jnp.exp(jax.random.uniform(key_piece, (TEMPLATES, SLOTS, 3, TLEN // 32, 1), jnp.float32, 0.0, math.log(3.0)))
    piece_gain = jnp.broadcast_to(piece_gain, (TEMPLATES, SLOTS, 3, TLEN // 32, 32)).reshape(TEMPLATES, SLOTS, 3, TLEN)
    return (values * channel_gain * piece_gain).astype(jnp.bfloat16)


def draw_station_ids(key, part):
    subkeys = jax.random.split(key, TEMPLATES // TPL_GROUP)

    def draw_group(group_key):
        key_anchor, key_weight, key_jitter, key_shuffle, key_rotate = jax.random.split(group_key, 5)
        blocks = SLOTS
        extent = SLOTS // 8
        anchor = jax.random.randint(key_anchor, (), 0, blocks)
        weight = jax.random.randint(key_weight, (blocks,), 0, 4)
        jitter = jax.random.randint(key_jitter, (blocks, CAP), 0, 4096)
        offset = (jnp.arange(blocks, dtype=jnp.int32) - anchor) % blocks
        is_hot = offset < extent
        scores = jnp.where(is_hot[:, None], 4 * 4096, weight[:, None] * 4096 + jitter)
        scores = scores * (blocks * CAP) + jnp.arange(blocks * CAP, dtype=jnp.int32).reshape(blocks, CAP)
        chosen = lax.top_k(scores.reshape(-1), TPL_GROUP)[1]
        shuffle = jax.random.permutation(key_shuffle, TPL_GROUP)
        centre = (chosen // CAP)[shuffle]
        rotate = jax.random.randint(key_rotate, (TPL_GROUP,), 0, STA_DEV)
        slot_ids = jnp.arange(SLOTS, dtype=jnp.int32)
        owners = (centre[:, None] + slot_ids[None, :] // 8) % blocks
        within = (rotate[:, None] + slot_ids[None, :] % 8) % STA_DEV
        return (owners * STA_DEV + within).astype(jnp.int32)
    return jax.vmap(draw_group)(subkeys).reshape(TEMPLATES, SLOTS)


def touch_ends(array, stream_key, low, high):
    spot = [jax.random.randint(jax.random.fold_in(stream_key, axis), (), 0, length) for axis, length in enumerate(array.shape)]
    main_axis = array.shape.index(max(array.shape))
    neighbour = spot[:main_axis] + [(spot[main_axis] + 1) % array.shape[main_axis]] + spot[main_axis + 1:]
    return array.at[tuple(spot)].set(low).at[tuple(neighbour)].set(high)


def setup_inputs(seed: int = 0) -> dict:
    key_of = jax.random.split(jax.random.key(seed), 5)
    records = draw_records(jax.random.fold_in(key_of[4], 71), 0)
    waveforms = draw_waveforms(jax.random.fold_in(key_of[4], 71), 0)
    station_ids = draw_station_ids(jax.random.fold_in(key_of[4], 71), 0)
    lag_steps = touch_ends(jax.random.randint(key_of[3], (TEMPLATES, SLOTS, 3), 0, MAXLAG), jax.random.fold_in(key_of[3], 1), 0, MAXLAG - 1).astype(jnp.int32)
    return dict(records=records, waveforms=waveforms, station_ids=station_ids, lag_steps=lag_steps)


epsilon = 1e-05

def window_scale(pieces):
    squares = pieces * pieces
    running = jnp.cumsum(squares, axis=-1)
    running = jnp.concatenate([jnp.zeros(running.shape[:-1] + (1,), running.dtype), running], axis=-1)
    return jnp.sqrt((running[..., TLEN:] - running[..., :-TLEN]) / TLEN + epsilon)

def reference(records, waveforms, station_ids, lag_steps):

    def cut_window(series, offset):
        return lax.dynamic_slice_in_dim(series, offset, WINDOW + TLEN - 1)

    def one_template(block_items):
        wave_rows, stations, offsets = block_items
        station_rows = jnp.take(records, stations.astype(jnp.int32), axis=0)
        pieces = jax.vmap(jax.vmap(cut_window))(station_rows, offsets.astype(jnp.int32)).astype(jnp.float32)
        kernels = wave_rows.astype(jnp.float32)
        transform_size = WINDOW + TLEN
        spectra = jnp.fft.rfft(pieces, n=transform_size, axis=-1) * jnp.conj(jnp.fft.rfft(kernels, n=transform_size, axis=-1))
        raw_terms = jnp.fft.irfft(spectra, n=transform_size, axis=-1)[..., :WINDOW]
        energy_scale = window_scale(pieces)
        template_scale = jnp.sqrt(lax.optimization_barrier(jnp.mean(kernels * kernels, axis=-1)) + epsilon)
        normed = raw_terms / (TLEN * energy_scale * template_scale[..., None])
        return lax.optimization_barrier(jnp.sum(normed, axis=(0, 1)))
    network_stack = lax.map(one_template, (waveforms, station_ids, lag_steps))
    return network_stack.astype(jnp.float32)
```

```python
import functools

import jax
import jax.numpy as jnp
from jax import lax
from jax.experimental import pallas as pl
from jax.experimental.pallas import tpu as pltpu
from jax.sharding import PartitionSpec as P

WINDOW = 512
EPSILON = 1e-05
BLOCKS = 64
STATIONS = 32
OWNERS = 4
PER_OWNER = STATIONS // OWNERS
GROUP = 96
CAP = 3
STEPS = 8
CHANNELS = 3
TLEN = 256
POSITIONS = 768
SAMPLES = 1024
ENTRIES = BLOCKS * CAP
ROWS = 32
PARTS = POSITIONS // 128
F32, BF16, I32 = jnp.float32, jnp.bfloat16, jnp.int32


def iota(shape, axis):
    return lax.broadcasted_iota(I32, shape, axis)


def ones_where(mask):
    return jnp.where(mask, 1.0, 0.0).astype(BF16)


def mm(left, right):
    return jnp.dot(left, right, preferred_element_type=F32)


def routing(block):
    hot = iota((BLOCKS, GROUP), 0) == block
    earlier = ones_where(iota((GROUP, GROUP), 0) < iota((GROUP, GROUP), 1))
    return hot, mm(ones_where(hot), earlier)


def pack_kernel(ids_ref, lag_ref, wave_ref, out_ref, rows_ref):
    me = lax.axis_index("tpl")
    ids = ids_ref[...]
    block = ids >> 5
    within = ids & (STATIONS - 1)
    label = ((me + OWNERS - (within >> 3)) & (OWNERS - 1)) * PER_OWNER + (within & (PER_OWNER - 1))
    hot, count = routing(block)
    kind = iota((128, GROUP), 0)
    details = jnp.where(kind == 0, label, 0)
    for channel in range(CHANNELS):
        details = jnp.where(kind == channel + 1, lag_ref[channel], details)
    details = details.astype(F32).astype(BF16)
    flip = ones_where(iota((TLEN, TLEN), 0) + iota((TLEN, TLEN), 1) == TLEN - 1)
    waves = [mm(wave_ref[channel], flip).astype(BF16) for channel in range(CHANNELS)]
    for c in range(CAP):
        pick = ones_where(hot & (count == float(c)))
        for channel in range(CHANNELS):
            part = mm(pick, waves[channel])
            for half in range(2):
                rows_ref[pl.ds(8 * c + 2 * channel + half, BLOCKS, stride=8 * CAP), :] = part[
                    :, 128 * half : 128 * half + 128
                ]
        rows_ref[pl.ds(8 * c + 6, BLOCKS, stride=8 * CAP), :] = lax.dot_general(
            pick, details, (((1,), (1,)), ((), ())), preferred_element_type=F32
        )
        rows_ref[pl.ds(8 * c + 7, BLOCKS, stride=8 * CAP), :] = jnp.zeros((BLOCKS, 128), F32)
    out_ref[...] = rows_ref[...].astype(BF16).reshape(BLOCKS, 8 * CAP, 128)


def correlate_kernel(
    got_ref,
    *refs,
):
    pieces = refs[:OWNERS]
    out_ref = refs[OWNERS]
    rows_ref, meta_ref, meta_smem, wave_ref, rec_ref, inv_ref, hankel_ref, raw_ref, scale_ref, acc_ref, sem = refs[OWNERS + 1 :]
    rows_ref[...] = got_ref[...].astype(F32).reshape(ENTRIES * 8, 128)

    details = rows_ref[pl.ds(6, ENTRIES, stride=8), :]
    details = jnp.concatenate([details, jnp.zeros((64, 128), F32)], axis=0).T
    meta_ref[...] = details[0:8].astype(I32)
    copy = pltpu.make_async_copy(meta_ref, meta_smem, sem)
    copy.start()

    entry = iota((1, ENTRIES), 1)
    source = entry // CAP
    key = details[0:1, :ENTRIES].astype(I32) * ROWS + (source >> 3) * 4 + (entry - source * CAP)
    select = ones_where(iota((STATIONS * ROWS, ENTRIES), 0) == key)
    for channel in range(CHANNELS):
        wave = jnp.concatenate(
            [rows_ref[pl.ds(2 * channel + half, ENTRIES, stride=8), :] for half in range(2)], axis=1
        )
        power = jnp.sum(wave * wave, axis=1, keepdims=True)
        scale = lax.rsqrt(power * (1.0 / TLEN) + EPSILON) * (1.0 / TLEN)
        scale_ref[channel] = jnp.broadcast_to(scale, (ENTRIES, 128))
        wave_ref[channel] = mm(select, wave.astype(BF16)).astype(BF16)

    delta = iota((2 * TLEN, TLEN), 0) - iota((2 * TLEN, TLEN), 1)
    band = ones_where((delta >= 0) & (delta < TLEN))
    for channel in range(CHANNELS):
        rec = jnp.concatenate([piece[channel].astype(F32) for piece in pieces], axis=0)
        rec_ref[channel * STATIONS : channel * STATIONS + STATIONS, :] = rec
        squares = rec * rec
        high = squares.astype(BF16)
        low = (squares - high.astype(F32)).astype(BF16)
        for part in range(POSITIONS // TLEN):
            lanes = slice(part * TLEN, part * TLEN + 2 * TLEN)
            energy = mm(high[:, lanes], band) + mm(low[:, lanes], band)
            inv_ref[channel * STATIONS : channel * STATIONS + STATIONS, part * TLEN : part * TLEN + TLEN] = lax.rsqrt(
                energy * (1.0 / TLEN) + EPSILON
            )

    def station_step(station, carry):
        for channel in range(CHANNELS):
            row = channel * STATIONS + station
            series = jnp.broadcast_to(rec_ref[pl.ds(row, 1), :], (16, SAMPLES))
            base = pltpu.roll(series, 1, 1, stride=1, stride_axis=0)
            for group in range(8):
                moved = (base if group == 0 else pltpu.roll(base, 16 * group, 1)).astype(BF16)
                hankel_ref[channel, 16 * group : 16 * group + 16, :] = moved[:, 256:]
                hankel_ref[channel, 128 + 16 * group : 128 + 16 * group + 16, :] = moved[:, 128:896]
            left = wave_ref[channel, pl.ds(pl.multiple_of(station * ROWS, ROWS), ROWS), :]
            raw = mm(left, hankel_ref[channel]) * inv_ref[pl.ds(row, 1), :]
            for part in range(PARTS):
                start = pl.multiple_of((row * PARTS + part) * ROWS, ROWS)
                raw_ref[pl.ds(start, ROWS), :] = raw[:, 128 * part : 128 * part + 128]
        return carry

    lax.fori_loop(0, STATIONS, station_step, 0)
    copy.wait()
    acc_ref[...] = jnp.zeros_like(acc_ref)
    lane = iota((4, 128), 1)

    def template_step(index, carry):
        step = index // CAP
        c = index - step * CAP
        place = step * 4 + c
        total = jnp.zeros((4, 128), F32)
        for slot in range(8):
            e = (step * 8 + slot) * CAP + c
            station = meta_smem[0, e]
            for channel in range(CHANNELS):
                lag = meta_smem[channel + 1, e]
                fine = lag & 127
                start = ((channel * STATIONS + station) * PARTS + (lag >> 7)) * ROWS + place
                here = raw_ref[pl.ds(start, 4, stride=ROWS), :]
                beyond = raw_ref[pl.ds(start + ROWS, 4, stride=ROWS), :]
                joined = jnp.where(lane >= fine, here, beyond) * scale_ref[channel, pl.ds(e, 1), :]
                total = total + pltpu.roll(joined, (128 - fine) & 127, 1)
        acc_ref[pl.ds(place, 4, stride=ROWS), :] = total
        return carry

    lax.fori_loop(0, STEPS * CAP, template_step, 0)
    acc_ref[...] = acc_ref[...].T
    quarter = iota((16, 128), 1) >> 5
    for half in range(2):
        columns = [acc_ref[pl.ds(4 * half + low, 16, stride=8), :] for low in range(4)]
        for part in range(4):
            joined = None
            for low in range(4):
                shift = (32 * (low - part)) % 128
                moved = columns[low] if shift == 0 else pltpu.roll(columns[low], shift, 1)
                joined = moved if joined is None else jnp.where(quarter == low, moved, joined)
            out_ref[16 * part : 16 * part + 16, half, :] = joined


def unpack_kernel(ids_ref, got_ref, out_ref, twice_ref):
    shift = lax.axis_index("sta") >> 3
    block = ((ids_ref[...] >> 5) + BLOCKS - shift) & (BLOCKS - 1)
    hot, count = routing(block)
    hot = jnp.where(hot, 1.0, 0.0)
    rank = jnp.sum(hot * count, axis=0, keepdims=True)
    step = (iota((BLOCKS, 128), 1) >> 2) & 7
    keep = (iota((128, GROUP), 0) & 3).astype(F32) == rank
    for half in range(2):
        twice_ref[0:BLOCKS, :] = got_ref[:, half, :]
        twice_ref[BLOCKS : 2 * BLOCKS, :] = got_ref[:, half, :]
        aligned = twice_ref[0:BLOCKS, :]
        for d in range(1, STEPS):
            aligned = jnp.where(step == d, twice_ref[d : d + BLOCKS, :], aligned)
        picked = jnp.dot(aligned.T, hot, precision=lax.Precision.HIGHEST, preferred_element_type=F32)
        picked = jnp.where(keep, picked, 0.0)
        for low in range(4):
            out_ref[4 * half + low : 4 * half + low + 1, :] = jnp.sum(
                picked[32 * low : 32 * low + 32], axis=0, keepdims=True
            )


VMEM = pl.BlockSpec(memory_space=pltpu.VMEM)


def on_device(records, waveforms, station_ids, lag_steps):
    ids = station_ids.T
    own = records.transpose(1, 0, 2)
    pieces = [own] + [
        lax.ppermute(own, "tpl", [(i, (i + hop) % OWNERS) for i in range(OWNERS)])
        for hop in range(1, OWNERS)
    ]
    send = pl.pallas_call(
        pack_kernel,
        out_shape=jax.ShapeDtypeStruct((BLOCKS, 8 * CAP, 128), BF16),
        in_specs=[VMEM] * 3,
        out_specs=VMEM,
        scratch_shapes=[pltpu.VMEM((BLOCKS * 8 * CAP, 128), F32)],
        name="pack",
    )(ids, lag_steps.transpose(2, 1, 0), waveforms[:, 0].transpose(1, 0, 2))
    got = lax.all_to_all(send, "sta", split_axis=0, concat_axis=0, tiled=True)
    stacks = pl.pallas_call(
        correlate_kernel,
        out_shape=jax.ShapeDtypeStruct((BLOCKS, 2, 128), F32),
        in_specs=[VMEM] * (1 + OWNERS),
        out_specs=VMEM,
        scratch_shapes=[
            pltpu.VMEM((ENTRIES * 8, 128), F32),
            pltpu.VMEM((8, 256), I32),
            pltpu.SMEM((8, 256), I32),
            pltpu.VMEM((CHANNELS, STATIONS * ROWS, TLEN), BF16),
            pltpu.VMEM((CHANNELS * STATIONS, SAMPLES), F32),
            pltpu.VMEM((CHANNELS * STATIONS, POSITIONS), F32),
            pltpu.VMEM((CHANNELS, TLEN, POSITIONS), BF16),
            pltpu.VMEM((CHANNELS * STATIONS * PARTS * ROWS, 128), F32),
            pltpu.VMEM((CHANNELS, ENTRIES, 128), F32),
            pltpu.VMEM((128, 128), F32),
            pltpu.SemaphoreType.DMA,
        ],
        compiler_params=pltpu.CompilerParams(vmem_limit_bytes=40 << 20),
        name="correlate",
    )(got, *pieces)
    shared = lax.all_to_all(stacks, "sta", split_axis=0, concat_axis=0, tiled=True)
    out = pl.pallas_call(
        unpack_kernel,
        out_shape=jax.ShapeDtypeStruct((8, GROUP), F32),
        in_specs=[VMEM] * 2,
        out_specs=VMEM,
        scratch_shapes=[pltpu.VMEM((2 * BLOCKS, 128), F32)],
        name="unpack",
    )(ids, shared)
    return out.T


def solution(mesh):
    in_specs = (
        P(("sta", "tpl"), None, None),
        P("tpl", "sta", None, None),
        P("tpl", "sta"),
        P("tpl", "sta", None),
    )
    return jax.shard_map(
        on_device, mesh=mesh, in_specs=in_specs, out_specs=P("tpl", "sta"), check_vma=False
    )
```

```python
import functools

import jax
import jax.numpy as jnp
from jax import lax
from jax.experimental import pallas as pl
from jax.experimental.pallas import tpu as pltpu
from jax.sharding import PartitionSpec as P

WINDOW = 512
EPSILON = 1e-05
BLOCKS = 64
STATIONS = 32
OWNERS = 4
PER_OWNER = STATIONS // OWNERS
GROUP = 96
CAP = 3
STEPS = 8
CHANNELS = 3
TLEN = 256
SAMPLES = 1024
ENTRIES = BLOCKS * CAP
ROWS = STEPS * CAP
PHASES = 8
LINES = 2 * PHASES - 1
SHIFTS = TLEN // PHASES
UNROLL = 8
SPLIT = 2
SPAN = PHASES // SPLIT
TAPS = TLEN // SPLIT
F32, BF16, I32 = jnp.float32, jnp.bfloat16, jnp.int32


def iota(shape, axis):
    return lax.broadcasted_iota(I32, shape, axis)


def ones_where(mask):
    return jnp.where(mask, 1.0, 0.0).astype(BF16)


def mm(left, right):
    return jnp.dot(left, right, preferred_element_type=F32)


def routing(block):
    hot = iota((BLOCKS, GROUP), 0) == block
    earlier = ones_where(iota((GROUP, GROUP), 0) < iota((GROUP, GROUP), 1))
    return hot, mm(ones_where(hot), earlier)


def pack_kernel(ids_ref, lag_ref, wave_ref, out_ref, rows_ref):
    me = lax.axis_index("tpl")
    ids = ids_ref[...]
    block = ids >> 5
    within = ids & (STATIONS - 1)
    label = ((me + OWNERS - (within >> 3)) & (OWNERS - 1)) * PER_OWNER + (within & (PER_OWNER - 1))
    hot, count = routing(block)
    kind = iota((128, GROUP), 0)
    column = iota((TLEN, TLEN), 1)
    order = ones_where(iota((TLEN, TLEN), 0) == 8 * (31 - (column & 31)) + (column >> 5))
    waves = [mm(wave_ref[channel], order).astype(BF16) for channel in range(CHANNELS)]
    shared = jnp.zeros((BLOCKS, 128), F32)
    for c in range(CAP):
        pick = ones_where(hot & (count == float(c)))
        for channel in range(CHANNELS):
            part = mm(pick, waves[channel])
            for half in range(2):
                rows_ref[pl.ds(6 * c + 2 * channel + half, BLOCKS, stride=24), :] = part[
                    :, 128 * half : 128 * half + 128
                ]
        details = jnp.where(kind == 8 * c, label, 0)
        for channel in range(CHANNELS):
            details = jnp.where(kind == 8 * c + channel + 1, lag_ref[channel], details)
        shared += lax.dot_general(
            pick, details.astype(F32).astype(BF16), (((1,), (1,)), ((), ())), preferred_element_type=F32
        )
    rows_ref[pl.ds(18, BLOCKS, stride=24), :] = shared
    rows_ref[pl.ds(19, BLOCKS, stride=24), :] = jnp.zeros((BLOCKS, 128), F32)
    rows = rows_ref[...].reshape(BLOCKS, 24, 128)
    for part in range(5):
        out_ref[:, part] = rows[:, 4 * part : 4 * part + 4].astype(BF16)


def prepare_kernel(*refs):
    pieces = refs[:OWNERS]
    out_ref = refs[OWNERS]
    rows = CHANNELS * STATIONS
    records = jnp.concatenate([piece[channel] for channel in range(CHANNELS) for piece in pieces], axis=0)
    column = iota((SAMPLES, SAMPLES), 1)
    order = ones_where(iota((SAMPLES, SAMPLES), 0) == 8 * (column & 127) + (column >> 7))
    phases = mm(records, order)
    squares = []
    for phase in range(PHASES):
        part = phases[:, 128 * phase : 128 * phase + 128]
        out_ref[0, pl.ds(phase, rows, stride=PHASES), :] = part
        squares.append(part * part)
    prefix = [jnp.zeros((rows, 128), F32)]
    for phase in range(PHASES):
        prefix.append(prefix[-1] + squares[phase])
    suffix = [squares[PHASES - 1]]
    for phase in range(PHASES - 2, -1, -1):
        suffix.append(suffix[-1] + squares[phase])
    suffix = suffix[::-1]
    delta = iota((128, 128), 0) - iota((128, 128), 1) + SHIFTS
    band = ones_where((delta >= 1) & (delta < SHIFTS))
    whole = prefix[PHASES]
    high = whole.astype(BF16)
    rest = whole - high.astype(F32)
    middle = rest.astype(BF16)
    low = (rest - middle.astype(F32)).astype(BF16)
    inner = mm(high, band) + (mm(middle, band) + mm(low, band))
    for phase in range(PHASES):
        energy = inner + (pltpu.roll(suffix[phase], SHIFTS, 1) + prefix[phase])
        out_ref[1, pl.ds(phase, rows, stride=PHASES), :] = lax.rsqrt(energy * (1.0 / TLEN) + EPSILON)


def correlate_kernel(
    got_ref, prepared_ref, out_ref, rows_ref, meta_ref, meta_smem, wave_ref, hankel_ref, raw_ref, scale_ref, acc_ref, sem
):
    got = got_ref[...].astype(F32)
    for part in range(5):
        rows_ref[:, 4 * part : 4 * part + 4, :] = got[:, part]
    rows = rows_ref.reshape(BLOCKS * 24, 128)

    details = rows[pl.ds(18, BLOCKS, stride=24), :]
    details = jnp.concatenate([details, jnp.zeros((BLOCKS, 128), F32)], axis=0).T.astype(I32)
    step = iota((1, 128), 1) >> 3
    keys = []
    for c in range(CAP):
        place = step * CAP + c
        station = details[8 * c : 8 * c + 1]
        keys.append((station * ROWS + place)[:, :BLOCKS])
        for channel in range(CHANNELS):
            lag = details[8 * c + channel + 1 : 8 * c + channel + 2]
            line = CHANNELS * c + channel
            meta_ref[line : line + 1, :] = (
                (channel * STATIONS + station) * LINES + (lag & 7)
            ) * ROWS + place
            meta_ref[line + 9 : line + 10, :] = 128 - SHIFTS - (lag >> 3)
    copy = pltpu.make_async_copy(meta_ref, meta_smem, sem)
    copy.start()

    select = ones_where(iota((STATIONS * ROWS, ENTRIES), 0) == jnp.concatenate(keys, axis=1))
    for channel in range(CHANNELS):
        wave = jnp.concatenate(
            [
                jnp.concatenate(
                    [rows[pl.ds(6 * c + 2 * channel + half, BLOCKS, stride=24), :] for half in range(2)], axis=1
                )
                for c in range(CAP)
            ],
            axis=0,
        )
        power = jnp.sum(wave * wave, axis=1, keepdims=True)
        scale = lax.rsqrt(power * (1.0 / TLEN) + EPSILON) * (1.0 / TLEN)
        scale_ref[channel] = jnp.broadcast_to(scale, (ENTRIES, 128))
        spread = mm(select, wave.astype(BF16)).astype(BF16).reshape(STATIONS, ROWS, TLEN)
        for group in range(SPLIT):
            wave_ref[channel, :, ROWS * group : ROWS * group + ROWS, :] = spread[:, :, TAPS * group : TAPS * group + TAPS]

    def station_step(turn, carry):
        for item in range(UNROLL * CHANNELS):
            channel = item % CHANNELS
            station = turn * UNROLL + item // CHANNELS
            row = channel * STATIONS + station
            first = pl.multiple_of(row * PHASES, PHASES)
            for phase in range(2 * PHASES - 1):
                series = jnp.broadcast_to(prepared_ref[0, pl.ds(first + phase % PHASES, 1), :], (SHIFTS, 128))
                moved = pltpu.roll(series, 1 if phase < PHASES else 0, 1, stride=1, stride_axis=0)
                hankel_ref[item, SHIFTS * phase : SHIFTS * phase + SHIFTS, :] = moved.astype(BF16)
            sums = [None] * PHASES
            for block in range(0, 2 * PHASES - SPAN, 2):
                groups = [g for g in range(SPLIT) if 0 <= block - SPAN * g < PHASES]
                right = jnp.concatenate(
                    [hankel_ref[item, SHIFTS * m : SHIFTS * m + TAPS, :] for m in (block, block + 1)], axis=1
                )
                both = mm(wave_ref[channel, station, ROWS * groups[0] : ROWS * (groups[-1] + 1), :], right)
                for index, g in enumerate(groups):
                    for side in range(2):
                        phase = block + side - SPAN * g
                        part = both[ROWS * index : ROWS * (index + 1), 128 * side : 128 * side + 128]
                        sums[phase] = part if sums[phase] is None else sums[phase] + part
                    if g < SPLIT - 1:
                        continue
                    for side in range(2):
                        phase = block + side - SPAN * g
                        raw = sums[phase] * prepared_ref[1, pl.ds(first + phase, 1), :]
                        start = pl.multiple_of((row * LINES + phase) * ROWS, 8)
                        raw_ref[pl.ds(start, ROWS), :] = raw
                        if phase < PHASES - 1:
                            start = pl.multiple_of((row * LINES + phase + PHASES) * ROWS, 8)
                            raw_ref[pl.ds(start, ROWS), :] = pltpu.roll(raw, 127, 1)
        return carry

    lax.fori_loop(0, STATIONS // UNROLL, station_step, 0)
    copy.wait()
    acc_ref[...] = jnp.zeros_like(acc_ref)

    def template_step(step, carry):
        for c in range(CAP):
            totals = [None, None]
            for slot in range(8):
                source = step * 8 + slot
                for channel in range(CHANNELS):
                    line = CHANNELS * c + channel
                    start = meta_smem[line, source]
                    scale = scale_ref[channel, pl.ds(c * BLOCKS + source, 1), :]
                    part = raw_ref[pl.ds(start, PHASES, stride=ROWS), :] * scale
                    part = pltpu.roll(part, meta_smem[line + 9, source], 1)
                    side = (slot * CHANNELS + channel) % 2
                    totals[side] = part if totals[side] is None else totals[side] + part
            acc_ref[pl.ds(pl.multiple_of((step * 4 + c) * PHASES, PHASES), PHASES), :] = totals[0] + totals[1]
        return carry

    lax.fori_loop(0, STEPS, template_step, 0)
    for half in range(2):
        out_ref[:, half, :] = acc_ref[128 * half : 128 * half + 128, :].T[:BLOCKS]


def unpack_kernel(ids_ref, got_ref, out_ref, twice_ref):
    shift = lax.axis_index("sta") >> 3
    block = ((ids_ref[...] >> 5) + BLOCKS - shift) & (BLOCKS - 1)
    hot, count = routing(block)
    hot = jnp.where(hot, 1.0, 0.0)
    rank = jnp.sum(hot * count, axis=0, keepdims=True)
    quarter = iota((BLOCKS, 128), 1) >> 5
    keep = ((iota((128, GROUP), 0) >> 3) & 3).astype(F32) == rank
    total = None
    for half in range(2):
        twice_ref[0:BLOCKS, :] = got_ref[:, half, :]
        twice_ref[BLOCKS : 2 * BLOCKS, :] = got_ref[:, half, :]
        aligned = twice_ref[4 * half : 4 * half + BLOCKS, :]
        for d in range(1, 4):
            aligned = jnp.where(quarter == d, twice_ref[4 * half + d : 4 * half + d + BLOCKS, :], aligned)
        picked = jnp.dot(aligned.T, hot, precision=lax.Precision.HIGHEST, preferred_element_type=F32)
        picked = jnp.where(keep, picked, 0.0)
        for group in range(16):
            part = picked[8 * group : 8 * group + 8]
            total = part if total is None else total + part
    out_ref[...] = total


VMEM = pl.BlockSpec(memory_space=pltpu.VMEM)


def on_device(records, waveforms, station_ids, lag_steps):
    ids = station_ids.T
    own = records.transpose(1, 0, 2)
    pieces = [own] + [
        lax.ppermute(own, "tpl", [(i, (i + hop) % OWNERS) for i in range(OWNERS)])
        for hop in range(1, OWNERS)
    ]
    send = pl.pallas_call(
        pack_kernel,
        out_shape=jax.ShapeDtypeStruct((BLOCKS, 5, 4, 128), BF16),
        in_specs=[VMEM] * 3,
        out_specs=VMEM,
        scratch_shapes=[pltpu.VMEM((BLOCKS * 24, 128), F32)],
        compiler_params=pltpu.CompilerParams(vmem_limit_bytes=8 << 20),
        name="pack",
    )(ids, lag_steps.transpose(2, 1, 0), waveforms[:, 0].transpose(1, 0, 2))
    got = lax.all_to_all(send, "sta", split_axis=0, concat_axis=0, tiled=True)
    prepared = pl.pallas_call(
        prepare_kernel,
        out_shape=jax.ShapeDtypeStruct((2, CHANNELS * STATIONS * PHASES, 128), F32),
        in_specs=[VMEM] * OWNERS,
        out_specs=VMEM,
        cost_estimate=pl.CostEstimate(flops=4 * 10**8, bytes_accessed=1 << 20, transcendentals=0),
        compiler_params=pltpu.CompilerParams(vmem_limit_bytes=16 << 20),
        name="prepare",
    )(*pieces)
    stacks = pl.pallas_call(
        correlate_kernel,
        out_shape=jax.ShapeDtypeStruct((BLOCKS, 2, 128), F32),
        in_specs=[VMEM] * 2,
        out_specs=VMEM,
        scratch_shapes=[
            pltpu.VMEM((BLOCKS, 24, 128), F32),
            pltpu.VMEM((24, 128), I32),
            pltpu.SMEM((24, 128), I32),
            pltpu.VMEM((CHANNELS, STATIONS, SPLIT * ROWS, TAPS), BF16),
            pltpu.VMEM((UNROLL * CHANNELS, SHIFTS * (2 * PHASES - 1), 128), BF16),
            pltpu.VMEM((CHANNELS * STATIONS * LINES * ROWS, 128), F32),
            pltpu.VMEM((CHANNELS, ENTRIES, 128), F32),
            pltpu.VMEM((4 * STEPS * PHASES, 128), F32),
            pltpu.SemaphoreType.DMA,
        ],
        compiler_params=pltpu.CompilerParams(vmem_limit_bytes=40 << 20),
        name="correlate",
    )(got, prepared)
    shared = lax.all_to_all(stacks, "sta", split_axis=0, concat_axis=0, tiled=True)
    out = pl.pallas_call(
        unpack_kernel,
        out_shape=jax.ShapeDtypeStruct((8, GROUP), F32),
        in_specs=[VMEM] * 2,
        out_specs=VMEM,
        scratch_shapes=[pltpu.VMEM((2 * BLOCKS, 128), F32)],
        compiler_params=pltpu.CompilerParams(vmem_limit_bytes=8 << 20),
        name="unpack",
    )(ids, shared)
    return out.T


def solution(mesh):
    in_specs = (
        P(("sta", "tpl"), None, None),
        P("tpl", "sta", None, None),
        P("tpl", "sta"),
        P("tpl", "sta", None),
    )
    return jax.shard_map(
        on_device, mesh=mesh, in_specs=in_specs, out_specs=P("tpl", "sta"), check_vma=False
    )
```

```python
import functools

import jax
import jax.numpy as jnp
from jax import lax
from jax.experimental import pallas as pl
from jax.experimental.pallas import tpu as pltpu
from jax.sharding import PartitionSpec as P

WINDOW = 512
EPSILON = 1e-05
BLOCKS = 64
STATIONS = 32
OWNERS = 4
PER_OWNER = STATIONS // OWNERS
GROUP = 96
CAP = 3
STEPS = 8
CHANNELS = 3
TLEN = 256
SAMPLES = 1024
ENTRIES = BLOCKS * CAP
ROWS = STEPS * CAP
PHASES = 8
LINES = 2 * PHASES - 1
SHIFTS = TLEN // PHASES
UNROLL = 8
SPLIT = 2
SPAN = PHASES // SPLIT
TAPS = TLEN // SPLIT
F32, BF16, I32 = jnp.float32, jnp.bfloat16, jnp.int32


def iota(shape, axis):
    return lax.broadcasted_iota(I32, shape, axis)


def ones_where(mask):
    return jnp.where(mask, 1.0, 0.0).astype(BF16)


def mm(left, right):
    return jnp.dot(left, right, preferred_element_type=F32)


def routing(block):
    hot = iota((BLOCKS, GROUP), 0) == block
    earlier = ones_where(iota((GROUP, GROUP), 0) < iota((GROUP, GROUP), 1))
    return hot, mm(ones_where(hot), earlier)


def pack_kernel(ids_ref, lag_ref, wave_ref, out_ref, rows_ref):
    me = lax.axis_index("tpl")
    ids = ids_ref[...]
    block = ids >> 5
    within = ids & (STATIONS - 1)
    label = ((me + OWNERS - (within >> 3)) & (OWNERS - 1)) * PER_OWNER + (within & (PER_OWNER - 1))
    hot, count = routing(block)
    kind = iota((128, GROUP), 0)
    column = iota((TLEN, TLEN), 1)
    order = ones_where(iota((TLEN, TLEN), 0) == 8 * (31 - (column & 31)) + (column >> 5))
    waves = [mm(wave_ref[channel], order).astype(BF16) for channel in range(CHANNELS)]
    shared = jnp.zeros((BLOCKS, 128), F32)
    for c in range(CAP):
        pick = ones_where(hot & (count == float(c)))
        for channel in range(CHANNELS):
            part = mm(pick, waves[channel])
            for half in range(2):
                rows_ref[pl.ds(6 * c + 2 * channel + half, BLOCKS, stride=24), :] = part[
                    :, 128 * half : 128 * half + 128
                ]
        details = jnp.where(kind == 8 * c, label, 0)
        for channel in range(CHANNELS):
            details = jnp.where(kind == 8 * c + channel + 1, lag_ref[channel], details)
        shared += lax.dot_general(
            pick, details.astype(F32).astype(BF16), (((1,), (1,)), ((), ())), preferred_element_type=F32
        )
    rows_ref[pl.ds(18, BLOCKS, stride=24), :] = shared
    rows_ref[pl.ds(19, BLOCKS, stride=24), :] = jnp.zeros((BLOCKS, 128), F32)
    rows = rows_ref[...].reshape(BLOCKS, 24, 128)
    for part in range(5):
        out_ref[:, part] = rows[:, 4 * part : 4 * part + 4].astype(BF16)


def prepare_kernel(*refs):
    pieces = refs[:OWNERS]
    out_ref = refs[OWNERS]
    rows = CHANNELS * STATIONS
    records = jnp.concatenate([piece[channel] for channel in range(CHANNELS) for piece in pieces], axis=0)
    column = iota((SAMPLES, SAMPLES), 1)
    order = ones_where(iota((SAMPLES, SAMPLES), 0) == 8 * (column & 127) + (column >> 7))
    phases = mm(records, order)
    squares = []
    for phase in range(PHASES):
        part = phases[:, 128 * phase : 128 * phase + 128]
        out_ref[0, pl.ds(phase, rows, stride=PHASES), :] = part
        squares.append(part * part)
    prefix = [jnp.zeros((rows, 128), F32)]
    for phase in range(PHASES):
        prefix.append(prefix[-1] + squares[phase])
    suffix = [squares[PHASES - 1]]
    for phase in range(PHASES - 2, -1, -1):
        suffix.append(suffix[-1] + squares[phase])
    suffix = suffix[::-1]
    delta = iota((128, 128), 0) - iota((128, 128), 1) + SHIFTS
    band = ones_where((delta >= 1) & (delta < SHIFTS))
    whole = prefix[PHASES]
    high = whole.astype(BF16)
    rest = whole - high.astype(F32)
    middle = rest.astype(BF16)
    low = (rest - middle.astype(F32)).astype(BF16)
    inner = mm(high, band) + (mm(middle, band) + mm(low, band))
    for phase in range(PHASES):
        energy = inner + (pltpu.roll(suffix[phase], SHIFTS, 1) + prefix[phase])
        out_ref[1, pl.ds(phase, rows, stride=PHASES), :] = lax.rsqrt(energy * (1.0 / TLEN) + EPSILON)


def correlate_kernel(
    got_ref, prepared_ref, out_ref, rows_ref, meta_ref, meta_smem, wave_ref, hankel_ref, raw_ref, scale_ref, acc_ref, sem
):
    got = got_ref[...].astype(F32)
    for part in range(5):
        rows_ref[:, 4 * part : 4 * part + 4, :] = got[:, part]
    rows = rows_ref.reshape(BLOCKS * 24, 128)

    details = rows[pl.ds(18, BLOCKS, stride=24), :]
    details = jnp.concatenate([details, jnp.zeros((BLOCKS, 128), F32)], axis=0).T.astype(I32)
    step = iota((1, 128), 1) >> 3
    keys = []
    for c in range(CAP):
        place = step * CAP + c
        station = details[8 * c : 8 * c + 1]
        keys.append((station * ROWS + place)[:, :BLOCKS])
        for channel in range(CHANNELS):
            lag = details[8 * c + channel + 1 : 8 * c + channel + 2]
            line = CHANNELS * c + channel
            meta_ref[line : line + 1, :] = (
                (channel * STATIONS + station) * LINES + (lag & 7)
            ) * ROWS + place
            meta_ref[line + 9 : line + 10, :] = 128 - SHIFTS - (lag >> 3)
    copy = pltpu.make_async_copy(meta_ref, meta_smem, sem)
    copy.start()

    select = ones_where(iota((STATIONS * ROWS, ENTRIES), 0) == jnp.concatenate(keys, axis=1))
    for channel in range(CHANNELS):
        wave = jnp.concatenate(
            [
                jnp.concatenate(
                    [rows[pl.ds(6 * c + 2 * channel + half, BLOCKS, stride=24), :] for half in range(2)], axis=1
                )
                for c in range(CAP)
            ],
            axis=0,
        )
        power = jnp.sum(wave * wave, axis=1, keepdims=True)
        scale = lax.rsqrt(power * (1.0 / TLEN) + EPSILON) * (1.0 / TLEN)
        scale_ref[channel] = jnp.broadcast_to(scale, (ENTRIES, 128))
        spread = mm(select, wave.astype(BF16)).astype(BF16).reshape(STATIONS, ROWS, TLEN)
        for group in range(SPLIT):
            wave_ref[channel, :, ROWS * group : ROWS * group + ROWS, :] = spread[:, :, TAPS * group : TAPS * group + TAPS]

    def station_step(turn, carry):
        for item in range(UNROLL * CHANNELS):
            channel = item % CHANNELS
            station = turn * UNROLL + item // CHANNELS
            row = channel * STATIONS + station
            first = pl.multiple_of(row * PHASES, PHASES)
            for phase in range(2 * PHASES - 1):
                series = jnp.broadcast_to(prepared_ref[0, pl.ds(first + phase % PHASES, 1), :], (SHIFTS, 128))
                moved = pltpu.roll(series, 1 if phase < PHASES else 0, 1, stride=1, stride_axis=0)
                hankel_ref[item, SHIFTS * phase : SHIFTS * phase + SHIFTS, :] = moved.astype(BF16)
            sums = [None] * PHASES
            for block in range(0, 2 * PHASES - SPAN, 2):
                groups = [g for g in range(SPLIT) if 0 <= block - SPAN * g < PHASES]
                right = jnp.concatenate(
                    [hankel_ref[item, SHIFTS * m : SHIFTS * m + TAPS, :] for m in (block, block + 1)], axis=1
                )
                both = mm(wave_ref[channel, station, ROWS * groups[0] : ROWS * (groups[-1] + 1), :], right)
                for index, g in enumerate(groups):
                    for side in range(2):
                        phase = block + side - SPAN * g
                        part = both[ROWS * index : ROWS * (index + 1), 128 * side : 128 * side + 128]
                        sums[phase] = part if sums[phase] is None else sums[phase] + part
                    if g < SPLIT - 1:
                        continue
                    for side in range(2):
                        phase = block + side - SPAN * g
                        raw = sums[phase] * prepared_ref[1, pl.ds(first + phase, 1), :]
                        start = pl.multiple_of((row * LINES + phase) * ROWS, 8)
                        raw_ref[pl.ds(start, ROWS), :] = raw
                        if phase < PHASES - 1:
                            start = pl.multiple_of((row * LINES + phase + PHASES) * ROWS, 8)
                            raw_ref[pl.ds(start, ROWS), :] = pltpu.roll(raw, 127, 1)
        return carry

    lax.fori_loop(0, STATIONS // UNROLL, station_step, 0, unroll=True)
    copy.wait()
    acc_ref[...] = jnp.zeros_like(acc_ref)

    def template_step(step, carry):
        for c in range(CAP):
            totals = [None, None]
            for slot in range(8):
                source = step * 8 + slot
                for channel in range(CHANNELS):
                    line = CHANNELS * c + channel
                    start = meta_smem[line, source]
                    scale = scale_ref[channel, pl.ds(c * BLOCKS + source, 1), :]
                    part = raw_ref[pl.ds(start, PHASES, stride=ROWS), :] * scale
                    part = pltpu.roll(part, meta_smem[line + 9, source], 1)
                    side = (slot * CHANNELS + channel) % 2
                    totals[side] = part if totals[side] is None else totals[side] + part
            acc_ref[pl.ds(pl.multiple_of((step * 4 + c) * PHASES, PHASES), PHASES), :] = totals[0] + totals[1]
        return carry

    lax.fori_loop(0, STEPS, template_step, 0, unroll=4)
    for half in range(2):
        out_ref[:, half, :] = acc_ref[128 * half : 128 * half + 128, :].T[:BLOCKS]


def unpack_kernel(ids_ref, got_ref, out_ref, twice_ref):
    shift = lax.axis_index("sta") >> 3
    block = ((ids_ref[...] >> 5) + BLOCKS - shift) & (BLOCKS - 1)
    hot, count = routing(block)
    hot = jnp.where(hot, 1.0, 0.0)
    rank = jnp.sum(hot * count, axis=0, keepdims=True)
    quarter = iota((BLOCKS, 128), 1) >> 5
    keep = ((iota((128, GROUP), 0) >> 3) & 3).astype(F32) == rank
    total = None
    for half in range(2):
        twice_ref[0:BLOCKS, :] = got_ref[:, half, :]
        twice_ref[BLOCKS : 2 * BLOCKS, :] = got_ref[:, half, :]
        aligned = twice_ref[4 * half : 4 * half + BLOCKS, :]
        for d in range(1, 4):
            aligned = jnp.where(quarter == d, twice_ref[4 * half + d : 4 * half + d + BLOCKS, :], aligned)
        picked = jnp.dot(aligned.T, hot, precision=lax.Precision.HIGHEST, preferred_element_type=F32)
        picked = jnp.where(keep, picked, 0.0)
        for group in range(16):
            part = picked[8 * group : 8 * group + 8]
            total = part if total is None else total + part
    out_ref[...] = total


VMEM = pl.BlockSpec(memory_space=pltpu.VMEM)


def on_device(records, waveforms, station_ids, lag_steps):
    ids = station_ids.T
    own = records.transpose(1, 0, 2)
    pieces = [own] + [
        lax.ppermute(own, "tpl", [(i, (i + hop) % OWNERS) for i in range(OWNERS)])
        for hop in range(1, OWNERS)
    ]
    send = pl.pallas_call(
        pack_kernel,
        out_shape=jax.ShapeDtypeStruct((BLOCKS, 5, 4, 128), BF16),
        in_specs=[VMEM] * 3,
        out_specs=VMEM,
        scratch_shapes=[pltpu.VMEM((BLOCKS * 24, 128), F32)],
        compiler_params=pltpu.CompilerParams(vmem_limit_bytes=60 << 20),
        name="pack",
    )(ids, lag_steps.transpose(2, 1, 0), waveforms[:, 0].transpose(1, 0, 2))
    got = lax.all_to_all(send, "sta", split_axis=0, concat_axis=0, tiled=True)
    prepared = pl.pallas_call(
        prepare_kernel,
        out_shape=jax.ShapeDtypeStruct((2, CHANNELS * STATIONS * PHASES, 128), F32),
        in_specs=[VMEM] * OWNERS,
        out_specs=VMEM,
        cost_estimate=pl.CostEstimate(flops=4 * 10**8, bytes_accessed=1 << 20, transcendentals=0),
        compiler_params=pltpu.CompilerParams(vmem_limit_bytes=16 << 20),
        name="prepare",
    )(*pieces)
    stacks = pl.pallas_call(
        correlate_kernel,
        out_shape=jax.ShapeDtypeStruct((BLOCKS, 2, 128), F32),
        in_specs=[VMEM] * 2,
        out_specs=VMEM,
        scratch_shapes=[
            pltpu.VMEM((BLOCKS, 24, 128), F32),
            pltpu.VMEM((24, 128), I32),
            pltpu.SMEM((24, 128), I32),
            pltpu.VMEM((CHANNELS, STATIONS, SPLIT * ROWS, TAPS), BF16),
            pltpu.VMEM((UNROLL * CHANNELS, SHIFTS * (2 * PHASES - 1), 128), BF16),
            pltpu.VMEM((CHANNELS * STATIONS * LINES * ROWS, 128), F32),
            pltpu.VMEM((CHANNELS, ENTRIES, 128), F32),
            pltpu.VMEM((4 * STEPS * PHASES, 128), F32),
            pltpu.SemaphoreType.DMA,
        ],
        compiler_params=pltpu.CompilerParams(vmem_limit_bytes=40 << 20),
        name="correlate",
    )(got, prepared)
    shared = lax.all_to_all(stacks, "sta", split_axis=0, concat_axis=0, tiled=True)
    out = pl.pallas_call(
        unpack_kernel,
        out_shape=jax.ShapeDtypeStruct((8, GROUP), F32),
        in_specs=[VMEM] * 2,
        out_specs=VMEM,
        scratch_shapes=[pltpu.VMEM((2 * BLOCKS, 128), F32)],
        compiler_params=pltpu.CompilerParams(vmem_limit_bytes=8 << 20),
        name="unpack",
    )(ids, shared)
    return out.T


def solution(mesh):
    in_specs = (
        P(("sta", "tpl"), None, None),
        P("tpl", "sta", None, None),
        P("tpl", "sta"),
        P("tpl", "sta", None),
    )
    return jax.shard_map(
        on_device, mesh=mesh, in_specs=in_specs, out_specs=P("tpl", "sta"), check_vma=False
    )
```

```python
import functools

import jax
import jax.numpy as jnp
from jax import lax
from jax.experimental import pallas as pl
from jax.experimental.pallas import tpu as pltpu
from jax.sharding import PartitionSpec as P

WINDOW = 512
EPSILON = 1e-05
BLOCKS = 64
STATIONS = 32
OWNERS = 4
PER_OWNER = STATIONS // OWNERS
GROUP = 96
CAP = 3
STEPS = 8
CHANNELS = 3
TLEN = 256
SAMPLES = 1024
ENTRIES = BLOCKS * CAP
ROWS = STEPS * CAP
PHASES = 8
LINES = 2 * PHASES - 1
SHIFTS = TLEN // PHASES
UNROLL = 8
SPLIT = 2
SPAN = PHASES // SPLIT
TAPS = TLEN // SPLIT
F32, BF16, I32 = jnp.float32, jnp.bfloat16, jnp.int32


def iota(shape, axis):
    return lax.broadcasted_iota(I32, shape, axis)


def ones_where(mask):
    return jnp.where(mask, 1.0, 0.0).astype(BF16)


def mm(left, right):
    return jnp.dot(left, right, preferred_element_type=F32)


def routing(block):
    hot = iota((BLOCKS, GROUP), 0) == block
    earlier = ones_where(iota((GROUP, GROUP), 0) < iota((GROUP, GROUP), 1))
    return hot, mm(ones_where(hot), earlier)


def pack_kernel(ids_ref, lag_ref, wave_ref, out_ref, rows_ref):
    me = lax.axis_index("tpl")
    ids = ids_ref[...]
    block = ids >> 5
    within = ids & (STATIONS - 1)
    label = ((me + OWNERS - (within >> 3)) & (OWNERS - 1)) * PER_OWNER + (within & (PER_OWNER - 1))
    hot, count = routing(block)
    kind = iota((128, GROUP), 0)
    column = iota((TLEN, TLEN), 1)
    order = ones_where(iota((TLEN, TLEN), 0) == 8 * (31 - (column & 31)) + (column >> 5))
    waves = [mm(wave_ref[channel], order).astype(BF16) for channel in range(CHANNELS)]
    shared = jnp.zeros((BLOCKS, 128), F32)
    for c in range(CAP):
        pick = ones_where(hot & (count == float(c)))
        for channel in range(CHANNELS):
            part = mm(pick, waves[channel])
            for half in range(2):
                rows_ref[pl.ds(6 * c + 2 * channel + half, BLOCKS, stride=24), :] = part[
                    :, 128 * half : 128 * half + 128
                ]
        details = jnp.where(kind == 8 * c, label, 0)
        for channel in range(CHANNELS):
            details = jnp.where(kind == 8 * c + channel + 1, lag_ref[channel], details)
        shared += lax.dot_general(
            pick, details.astype(F32).astype(BF16), (((1,), (1,)), ((), ())), preferred_element_type=F32
        )
    rows_ref[pl.ds(18, BLOCKS, stride=24), :] = shared
    rows_ref[pl.ds(19, BLOCKS, stride=24), :] = jnp.zeros((BLOCKS, 128), F32)
    rows = rows_ref[...].reshape(BLOCKS, 24, 128)
    for part in range(5):
        out_ref[:, part] = rows[:, 4 * part : 4 * part + 4].astype(BF16)


def prepare_kernel(*refs):
    pieces = refs[:OWNERS]
    out_ref = refs[OWNERS]
    rows = CHANNELS * STATIONS
    records = jnp.concatenate([piece[channel] for channel in range(CHANNELS) for piece in pieces], axis=0)
    column = iota((SAMPLES, SAMPLES), 1)
    order = ones_where(iota((SAMPLES, SAMPLES), 0) == 8 * (column & 127) + (column >> 7))
    phases = mm(records, order)
    squares = []
    for phase in range(PHASES):
        part = phases[:, 128 * phase : 128 * phase + 128]
        out_ref[0, pl.ds(phase, rows, stride=PHASES), :] = part
        squares.append(part * part)
    prefix = [jnp.zeros((rows, 128), F32)]
    for phase in range(PHASES):
        prefix.append(prefix[-1] + squares[phase])
    suffix = [squares[PHASES - 1]]
    for phase in range(PHASES - 2, -1, -1):
        suffix.append(suffix[-1] + squares[phase])
    suffix = suffix[::-1]
    delta = iota((128, 128), 0) - iota((128, 128), 1) + SHIFTS
    band = ones_where((delta >= 1) & (delta < SHIFTS))
    whole = prefix[PHASES]
    high = whole.astype(BF16)
    rest = whole - high.astype(F32)
    middle = rest.astype(BF16)
    low = (rest - middle.astype(F32)).astype(BF16)
    inner = mm(high, band) + (mm(middle, band) + mm(low, band))
    for phase in range(PHASES):
        energy = inner + (pltpu.roll(suffix[phase], SHIFTS, 1) + prefix[phase])
        out_ref[1, pl.ds(phase, rows, stride=PHASES), :] = lax.rsqrt(energy * (1.0 / TLEN) + EPSILON)


def correlate_kernel(
    got_ref, prepared_ref, out_ref, rows_ref, meta_ref, meta_smem, wave_ref, hankel_ref, raw_ref, scale_ref, acc_ref, sem
):
    got = got_ref[...].astype(F32)
    for part in range(5):
        rows_ref[:, 4 * part : 4 * part + 4, :] = got[:, part]
    rows = rows_ref.reshape(BLOCKS * 24, 128)

    details = rows[pl.ds(18, BLOCKS, stride=24), :]
    details = jnp.concatenate([details, jnp.zeros((BLOCKS, 128), F32)], axis=0).T.astype(I32)
    step = iota((1, 128), 1) >> 3
    keys = []
    for c in range(CAP):
        place = step * CAP + c
        station = details[8 * c : 8 * c + 1]
        keys.append((station * ROWS + place)[:, :BLOCKS])
        for channel in range(CHANNELS):
            lag = details[8 * c + channel + 1 : 8 * c + channel + 2]
            line = CHANNELS * c + channel
            meta_ref[line : line + 1, :] = (
                (channel * STATIONS + station) * LINES + (lag & 7)
            ) * ROWS + place
            meta_ref[line + 9 : line + 10, :] = 128 - SHIFTS - (lag >> 3)
    copy = pltpu.make_async_copy(meta_ref, meta_smem, sem)
    copy.start()

    select = ones_where(iota((STATIONS * ROWS, ENTRIES), 0) == jnp.concatenate(keys, axis=1))
    for channel in range(CHANNELS):
        wave = jnp.concatenate(
            [
                jnp.concatenate(
                    [rows[pl.ds(6 * c + 2 * channel + half, BLOCKS, stride=24), :] for half in range(2)], axis=1
                )
                for c in range(CAP)
            ],
            axis=0,
        )
        power = jnp.sum(wave * wave, axis=1, keepdims=True)
        scale = lax.rsqrt(power * (1.0 / TLEN) + EPSILON) * (1.0 / TLEN)
        scale_ref[channel] = jnp.broadcast_to(scale, (ENTRIES, 128))
        spread = mm(select, wave.astype(BF16)).astype(BF16).reshape(STATIONS, ROWS, TLEN)
        for group in range(SPLIT):
            wave_ref[channel, :, ROWS * group : ROWS * group + ROWS, :] = spread[:, :, TAPS * group : TAPS * group + TAPS]

    def station_step(turn, carry):
        for item in range(UNROLL * CHANNELS):
            channel = item % CHANNELS
            station = turn * UNROLL + item // CHANNELS
            row = channel * STATIONS + station
            first = pl.multiple_of(row * PHASES, PHASES)
            for phase in range(2 * PHASES - 1):
                series = jnp.broadcast_to(prepared_ref[0, pl.ds(first + phase % PHASES, 1), :], (SHIFTS, 128))
                moved = pltpu.roll(series, 1 if phase < PHASES else 0, 1, stride=1, stride_axis=0)
                hankel_ref[item, SHIFTS * phase : SHIFTS * phase + SHIFTS, :] = moved.astype(BF16)
            sums = [None] * PHASES
            for block in range(0, 2 * PHASES - SPAN, 2):
                groups = [g for g in range(SPLIT) if 0 <= block - SPAN * g < PHASES]
                right = jnp.concatenate(
                    [hankel_ref[item, SHIFTS * m : SHIFTS * m + TAPS, :] for m in (block, block + 1)], axis=1
                )
                both = mm(wave_ref[channel, station, ROWS * groups[0] : ROWS * (groups[-1] + 1), :], right)
                for index, g in enumerate(groups):
                    for side in range(2):
                        phase = block + side - SPAN * g
                        part = both[ROWS * index : ROWS * (index + 1), 128 * side : 128 * side + 128]
                        sums[phase] = part if sums[phase] is None else sums[phase] + part
                    if g < SPLIT - 1:
                        continue
                    for side in range(2):
                        phase = block + side - SPAN * g
                        raw = sums[phase] * prepared_ref[1, pl.ds(first + phase, 1), :]
                        start = pl.multiple_of((row * LINES + phase) * ROWS, 8)
                        raw_ref[pl.ds(start, ROWS), :] = raw
                        if phase < PHASES - 1:
                            start = pl.multiple_of((row * LINES + phase + PHASES) * ROWS, 8)
                            raw_ref[pl.ds(start, ROWS), :] = pltpu.roll(raw, 127, 1)
        return carry

    lax.fori_loop(0, STATIONS // UNROLL, station_step, 0, unroll=True)
    copy.wait()
    acc_ref[...] = jnp.zeros_like(acc_ref)

    def template_step(step, carry):
        for c in range(CAP):
            totals = [None, None]
            for slot in range(8):
                source = step * 8 + slot
                for channel in range(CHANNELS):
                    line = CHANNELS * c + channel
                    start = meta_smem[line, source]
                    scale = scale_ref[channel, pl.ds(c * BLOCKS + source, 1), :]
                    part = raw_ref[pl.ds(start, PHASES, stride=ROWS), :] * scale
                    part = pltpu.roll(part, meta_smem[line + 9, source], 1)
                    side = (slot * CHANNELS + channel) % 2
                    totals[side] = part if totals[side] is None else totals[side] + part
            acc_ref[pl.ds(pl.multiple_of((step * 4 + c) * PHASES, PHASES), PHASES), :] = totals[0] + totals[1]
        return carry

    lax.fori_loop(0, STEPS, template_step, 0, unroll=4)
    for half in range(2):
        out_ref[:, half, :] = acc_ref[128 * half : 128 * half + 128, :].T[:BLOCKS]


def unpack_kernel(ids_ref, got_ref, out_ref, twice_ref):
    shift = lax.axis_index("sta") >> 3
    block = ((ids_ref[...] >> 5) + BLOCKS - shift) & (BLOCKS - 1)
    hot, count = routing(block)
    hot = jnp.where(hot, 1.0, 0.0)
    rank = jnp.sum(hot * count, axis=0, keepdims=True)
    quarter = iota((BLOCKS, 128), 1) >> 5
    keep = ((iota((128, GROUP), 0) >> 3) & 3).astype(F32) == rank
    total = None
    for half in range(2):
        twice_ref[0:BLOCKS, :] = got_ref[:, half, :]
        twice_ref[BLOCKS : 2 * BLOCKS, :] = got_ref[:, half, :]
        aligned = twice_ref[4 * half : 4 * half + BLOCKS, :]
        for d in range(1, 4):
            aligned = jnp.where(quarter == d, twice_ref[4 * half + d : 4 * half + d + BLOCKS, :], aligned)
        picked = jnp.dot(aligned.T, hot, precision=lax.Precision.HIGHEST, preferred_element_type=F32)
        picked = jnp.where(keep, picked, 0.0)
        for group in range(16):
            part = picked[8 * group : 8 * group + 8]
            total = part if total is None else total + part
    out_ref[...] = total


VMEM = pl.BlockSpec(memory_space=pltpu.VMEM)


def on_device(records, waveforms, station_ids, lag_steps):
    ids = station_ids.T
    own = records.transpose(1, 0, 2)
    pieces = [own] + [
        lax.ppermute(own, "tpl", [(i, (i + hop) % OWNERS) for i in range(OWNERS)])
        for hop in range(1, OWNERS)
    ]
    send = pl.pallas_call(
        pack_kernel,
        out_shape=jax.ShapeDtypeStruct((BLOCKS, 5, 4, 128), BF16),
        in_specs=[VMEM] * 3,
        out_specs=VMEM,
        scratch_shapes=[pltpu.VMEM((BLOCKS * 24, 128), F32)],
        compiler_params=pltpu.CompilerParams(vmem_limit_bytes=60 << 20),
        name="pack",
    )(ids, lag_steps.transpose(2, 1, 0), waveforms[:, 0].transpose(1, 0, 2))
    got = lax.all_to_all(send, "sta", split_axis=0, concat_axis=0, tiled=True)
    prepared = pl.pallas_call(
        prepare_kernel,
        out_shape=jax.ShapeDtypeStruct((2, CHANNELS * STATIONS * PHASES, 128), F32),
        in_specs=[VMEM] * OWNERS,
        out_specs=VMEM,
        cost_estimate=pl.CostEstimate(flops=4 * 10**8, bytes_accessed=1 << 20, transcendentals=0),
        compiler_params=pltpu.CompilerParams(vmem_limit_bytes=16 << 20),
        name="prepare",
    )(*pieces)
    stacks = pl.pallas_call(
        correlate_kernel,
        out_shape=jax.ShapeDtypeStruct((BLOCKS, 2, 128), F32),
        in_specs=[VMEM] * 2,
        out_specs=VMEM,
        scratch_shapes=[
            pltpu.VMEM((BLOCKS, 24, 128), F32),
            pltpu.VMEM((24, 128), I32),
            pltpu.SMEM((24, 128), I32),
            pltpu.VMEM((CHANNELS, STATIONS, SPLIT * ROWS, TAPS), BF16),
            pltpu.VMEM((UNROLL * CHANNELS, SHIFTS * (2 * PHASES - 1), 128), BF16),
            pltpu.VMEM(((CHANNELS * STATIONS * LINES + 1) * ROWS, 128), F32),
            pltpu.VMEM((CHANNELS, ENTRIES, 128), F32),
            pltpu.VMEM((4 * STEPS * PHASES, 128), F32),
            pltpu.SemaphoreType.DMA,
        ],
        compiler_params=pltpu.CompilerParams(vmem_limit_bytes=40 << 20),
        name="correlate",
    )(got, prepared)
    shared = lax.all_to_all(stacks, "sta", split_axis=0, concat_axis=0, tiled=True)
    out = pl.pallas_call(
        unpack_kernel,
        out_shape=jax.ShapeDtypeStruct((8, GROUP), F32),
        in_specs=[VMEM] * 2,
        out_specs=VMEM,
        scratch_shapes=[pltpu.VMEM((2 * BLOCKS, 128), F32)],
        compiler_params=pltpu.CompilerParams(vmem_limit_bytes=8 << 20),
        name="unpack",
    )(ids, shared)
    return out.T


def solution(mesh):
    in_specs = (
        P(("sta", "tpl"), None, None),
        P("tpl", "sta", None, None),
        P("tpl", "sta"),
        P("tpl", "sta", None),
    )
    return jax.shard_map(
        on_device, mesh=mesh, in_specs=in_specs, out_specs=P("tpl", "sta"), check_vma=False
    )
```

```python
import functools

import jax
import jax.numpy as jnp
from jax import lax
from jax.experimental import pallas as pl
from jax.experimental.pallas import tpu as pltpu
from jax.sharding import PartitionSpec as P

WINDOW = 512
EPSILON = 1e-05
BLOCKS = 64
STATIONS = 32
OWNERS = 4
PER_OWNER = STATIONS // OWNERS
GROUP = 96
CAP = 3
STEPS = 8
CHANNELS = 3
TLEN = 256
SAMPLES = 1024
ENTRIES = BLOCKS * CAP
ROWS = STEPS * CAP
PHASES = 8
LINES = 2 * PHASES - 1
SHIFTS = TLEN // PHASES
UNROLL = 8
SPLIT = 2
SPAN = PHASES // SPLIT
TAPS = TLEN // SPLIT
F32, BF16, I32 = jnp.float32, jnp.bfloat16, jnp.int32


def iota(shape, axis):
    return lax.broadcasted_iota(I32, shape, axis)


def ones_where(mask):
    return jnp.where(mask, 1.0, 0.0).astype(BF16)


def mm(left, right):
    return jnp.dot(left, right, preferred_element_type=F32)


def routing(block):
    hot = iota((BLOCKS, GROUP), 0) == block
    earlier = ones_where(iota((GROUP, GROUP), 0) < iota((GROUP, GROUP), 1))
    return hot, mm(ones_where(hot), earlier)


def pack_kernel(ids_ref, lag_ref, wave_ref, out_ref, rows_ref):
    me = lax.axis_index("tpl")
    ids = ids_ref[...]
    block = ids >> 5
    within = ids & (STATIONS - 1)
    label = ((me + OWNERS - (within >> 3)) & (OWNERS - 1)) * PER_OWNER + (within & (PER_OWNER - 1))
    hot, count = routing(block)
    kind = iota((128, GROUP), 0)
    column = iota((TLEN, TLEN), 1)
    order = ones_where(iota((TLEN, TLEN), 0) == 8 * (31 - (column & 31)) + (column >> 5))
    waves = [mm(wave_ref[channel], order).astype(BF16) for channel in range(CHANNELS)]
    shared = jnp.zeros((BLOCKS, 128), F32)
    for c in range(CAP):
        pick = ones_where(hot & (count == float(c)))
        for channel in range(CHANNELS):
            part = mm(pick, waves[channel])
            for half in range(2):
                rows_ref[pl.ds(6 * c + 2 * channel + half, BLOCKS, stride=24), :] = part[
                    :, 128 * half : 128 * half + 128
                ]
        details = jnp.where(kind == 8 * c, label, 0)
        for channel in range(CHANNELS):
            details = jnp.where(kind == 8 * c + channel + 1, lag_ref[channel], details)
        shared += lax.dot_general(
            pick, details.astype(F32).astype(BF16), (((1,), (1,)), ((), ())), preferred_element_type=F32
        )
    rows_ref[pl.ds(18, BLOCKS, stride=24), :] = shared
    rows_ref[pl.ds(19, BLOCKS, stride=24), :] = jnp.zeros((BLOCKS, 128), F32)
    rows = rows_ref[...].reshape(BLOCKS, 24, 128)
    for part in range(5):
        out_ref[:, part] = rows[:, 4 * part : 4 * part + 4].astype(BF16)


def prepare_kernel(*refs):
    pieces = refs[:OWNERS]
    out_ref = refs[OWNERS]
    rows = CHANNELS * STATIONS
    records = jnp.concatenate([piece[channel] for channel in range(CHANNELS) for piece in pieces], axis=0)
    column = iota((SAMPLES, SAMPLES), 1)
    order = ones_where(iota((SAMPLES, SAMPLES), 0) == 8 * (column & 127) + (column >> 7))
    phases = mm(records, order)
    squares = []
    for phase in range(PHASES):
        part = phases[:, 128 * phase : 128 * phase + 128]
        out_ref[0, pl.ds(phase, rows, stride=PHASES), :] = part
        squares.append(part * part)
    prefix = [jnp.zeros((rows, 128), F32)]
    for phase in range(PHASES):
        prefix.append(prefix[-1] + squares[phase])
    suffix = [squares[PHASES - 1]]
    for phase in range(PHASES - 2, -1, -1):
        suffix.append(suffix[-1] + squares[phase])
    suffix = suffix[::-1]
    delta = iota((128, 128), 0) - iota((128, 128), 1) + SHIFTS
    band = ones_where((delta >= 1) & (delta < SHIFTS))
    whole = prefix[PHASES]
    high = whole.astype(BF16)
    rest = whole - high.astype(F32)
    middle = rest.astype(BF16)
    low = (rest - middle.astype(F32)).astype(BF16)
    inner = mm(high, band) + (mm(middle, band) + mm(low, band))
    for phase in range(PHASES):
        energy = inner + (pltpu.roll(suffix[phase], SHIFTS, 1) + prefix[phase])
        out_ref[1, pl.ds(phase, rows, stride=PHASES), :] = lax.rsqrt(energy * (1.0 / TLEN) + EPSILON)


def correlate_kernel(
    got_ref, prepared_ref, out_ref, rows_ref, meta_ref, meta_smem, wave_ref, hankel_ref, raw_ref, scale_ref, acc_ref, sem
):
    got = got_ref[...].astype(F32)
    for part in range(5):
        rows_ref[:, 4 * part : 4 * part + 4, :] = got[:, part]
    rows = rows_ref.reshape(BLOCKS * 24, 128)

    details = rows[pl.ds(18, BLOCKS, stride=24), :]
    details = jnp.concatenate([details, jnp.zeros((BLOCKS, 128), F32)], axis=0).T.astype(I32)
    step = iota((1, 128), 1) >> 3
    keys = []
    for c in range(CAP):
        place = step * CAP + c
        station = details[8 * c : 8 * c + 1]
        keys.append((station * ROWS + place)[:, :BLOCKS])
        for channel in range(CHANNELS):
            lag = details[8 * c + channel + 1 : 8 * c + channel + 2]
            line = CHANNELS * c + channel
            meta_ref[line : line + 1, :] = (
                (channel * STATIONS + station) * LINES + (lag & 7)
            ) * ROWS + place
            meta_ref[line + 9 : line + 10, :] = 128 - SHIFTS - (lag >> 3)
    copy = pltpu.make_async_copy(meta_ref, meta_smem, sem)
    copy.start()

    select = ones_where(iota((STATIONS * ROWS, ENTRIES), 0) == jnp.concatenate(keys, axis=1))
    for channel in range(CHANNELS):
        wave = jnp.concatenate(
            [
                jnp.concatenate(
                    [rows[pl.ds(6 * c + 2 * channel + half, BLOCKS, stride=24), :] for half in range(2)], axis=1
                )
                for c in range(CAP)
            ],
            axis=0,
        )
        power = jnp.sum(wave * wave, axis=1, keepdims=True)
        scale = lax.rsqrt(power * (1.0 / TLEN) + EPSILON) * (1.0 / TLEN)
        scale_ref[channel] = jnp.broadcast_to(scale, (ENTRIES, 128))
        spread = mm(select, wave.astype(BF16)).astype(BF16).reshape(STATIONS, ROWS, TLEN)
        for group in range(SPLIT):
            wave_ref[channel, :, ROWS * group : ROWS * group + ROWS, :] = spread[:, :, TAPS * group : TAPS * group + TAPS]

    def station_step(turn, carry):
        for item in range(UNROLL * CHANNELS):
            channel = item % CHANNELS
            station = turn * UNROLL + item // CHANNELS
            row = channel * STATIONS + station
            first = pl.multiple_of(row * PHASES, PHASES)
            for phase in range(2 * PHASES - 1):
                series = jnp.broadcast_to(prepared_ref[0, pl.ds(first + phase % PHASES, 1), :], (SHIFTS, 128))
                moved = pltpu.roll(series, 1 if phase < PHASES else 0, 1, stride=1, stride_axis=0)
                hankel_ref[item, SHIFTS * phase : SHIFTS * phase + SHIFTS, :] = moved.astype(BF16)
            sums = [None] * PHASES
            for block in range(0, 2 * PHASES - SPAN, 2):
                groups = [g for g in range(SPLIT) if 0 <= block - SPAN * g < PHASES]
                right = jnp.concatenate(
                    [hankel_ref[item, SHIFTS * m : SHIFTS * m + TAPS, :] for m in (block, block + 1)], axis=1
                )
                both = mm(wave_ref[channel, station, ROWS * groups[0] : ROWS * (groups[-1] + 1), :], right)
                for index, g in enumerate(groups):
                    for side in range(2):
                        phase = block + side - SPAN * g
                        part = both[ROWS * index : ROWS * (index + 1), 128 * side : 128 * side + 128]
                        sums[phase] = part if sums[phase] is None else sums[phase] + part
                    if g < SPLIT - 1:
                        continue
                    for side in range(2):
                        phase = block + side - SPAN * g
                        raw = sums[phase] * prepared_ref[1, pl.ds(first + phase, 1), :]
                        start = pl.multiple_of((row * LINES + phase) * ROWS, 8)
                        raw_ref[pl.ds(start, ROWS), :] = raw
                        if phase < PHASES - 1:
                            start = pl.multiple_of((row * LINES + phase + PHASES) * ROWS, 8)
                            raw_ref[pl.ds(start, ROWS), :] = pltpu.roll(raw, 127, 1)
        return carry

    lax.fori_loop(0, STATIONS // UNROLL, station_step, 0, unroll=True)
    copy.wait()
    acc_ref[...] = jnp.zeros_like(acc_ref)

    def template_step(step, carry):
        for c in range(CAP):
            totals = [None, None]
            for slot in range(8):
                source = step * 8 + slot
                for channel in range(CHANNELS):
                    line = CHANNELS * c + channel
                    start = meta_smem[line, source]
                    scale = scale_ref[channel, pl.ds(c * BLOCKS + source, 1), :]
                    part = raw_ref[pl.ds(start, PHASES, stride=ROWS), :] * scale
                    part = pltpu.roll(part, meta_smem[line + 9, source], 1)
                    side = (slot * CHANNELS + channel) % 2
                    totals[side] = part if totals[side] is None else totals[side] + part
            acc_ref[pl.ds(pl.multiple_of((step * 4 + c) * PHASES, PHASES), PHASES), :] = totals[0] + totals[1]
        return carry

    lax.fori_loop(0, STEPS, template_step, 0, unroll=True)
    for half in range(2):
        out_ref[:, half, :] = acc_ref[128 * half : 128 * half + 128, :].T[:BLOCKS]


def unpack_kernel(ids_ref, got_ref, out_ref, twice_ref):
    shift = lax.axis_index("sta") >> 3
    block = ((ids_ref[...] >> 5) + BLOCKS - shift) & (BLOCKS - 1)
    hot, count = routing(block)
    narrow = ones_where(hot)
    hot = jnp.where(hot, 1.0, 0.0)
    rank = jnp.sum(hot * count, axis=0, keepdims=True)
    quarter = iota((BLOCKS, 128), 1) >> 5
    keep = ((iota((128, GROUP), 0) >> 3) & 3).astype(F32) == rank
    total = None
    for half in range(2):
        twice_ref[0:BLOCKS, :] = got_ref[:, half, :]
        twice_ref[BLOCKS : 2 * BLOCKS, :] = got_ref[:, half, :]
        aligned = twice_ref[4 * half : 4 * half + BLOCKS, :]
        for d in range(1, 4):
            aligned = jnp.where(quarter == d, twice_ref[4 * half + d : 4 * half + d + BLOCKS, :], aligned)
        aligned = aligned.T
        high = aligned.astype(BF16)
        rest = aligned - high.astype(F32)
        middle = rest.astype(BF16)
        low = (rest - middle.astype(F32)).astype(BF16)
        picked = mm(high, narrow) + (mm(middle, narrow) + mm(low, narrow))
        picked = jnp.where(keep, picked, 0.0)
        for group in range(16):
            part = picked[8 * group : 8 * group + 8]
            total = part if total is None else total + part
    out_ref[...] = total


VMEM = pl.BlockSpec(memory_space=pltpu.VMEM)


def on_device(records, waveforms, station_ids, lag_steps):
    ids = station_ids.T
    own = records.transpose(1, 0, 2)
    pieces = [own] + [
        lax.ppermute(own, "tpl", [(i, (i + hop) % OWNERS) for i in range(OWNERS)])
        for hop in range(1, OWNERS)
    ]
    send = pl.pallas_call(
        pack_kernel,
        out_shape=jax.ShapeDtypeStruct((BLOCKS, 5, 4, 128), BF16),
        in_specs=[VMEM] * 3,
        out_specs=VMEM,
        scratch_shapes=[pltpu.VMEM((BLOCKS * 24, 128), F32)],
        compiler_params=pltpu.CompilerParams(vmem_limit_bytes=60 << 20),
        name="pack",
    )(ids, lag_steps.transpose(2, 1, 0), waveforms[:, 0].transpose(1, 0, 2))
    got = lax.all_to_all(send, "sta", split_axis=0, concat_axis=0, tiled=True)
    prepared = pl.pallas_call(
        prepare_kernel,
        out_shape=jax.ShapeDtypeStruct((2, CHANNELS * STATIONS * PHASES, 128), F32),
        in_specs=[VMEM] * OWNERS,
        out_specs=VMEM,
        cost_estimate=pl.CostEstimate(flops=4 * 10**8, bytes_accessed=1 << 20, transcendentals=0),
        compiler_params=pltpu.CompilerParams(vmem_limit_bytes=16 << 20),
        name="prepare",
    )(*pieces)
    stacks = pl.pallas_call(
        correlate_kernel,
        out_shape=jax.ShapeDtypeStruct((BLOCKS, 2, 128), F32),
        in_specs=[VMEM] * 2,
        out_specs=VMEM,
        scratch_shapes=[
            pltpu.VMEM((BLOCKS, 24, 128), F32),
            pltpu.VMEM((24, 128), I32),
            pltpu.SMEM((24, 128), I32),
            pltpu.VMEM((CHANNELS, STATIONS, SPLIT * ROWS, TAPS), BF16),
            pltpu.VMEM((UNROLL * CHANNELS, SHIFTS * (2 * PHASES - 1), 128), BF16),
            pltpu.VMEM(((CHANNELS * STATIONS * LINES + 1) * ROWS, 128), F32),
            pltpu.VMEM((CHANNELS, ENTRIES, 128), F32),
            pltpu.VMEM((4 * STEPS * PHASES, 128), F32),
            pltpu.SemaphoreType.DMA,
        ],
        compiler_params=pltpu.CompilerParams(vmem_limit_bytes=40 << 20),
        name="correlate",
    )(got, prepared)
    shared = lax.all_to_all(stacks, "sta", split_axis=0, concat_axis=0, tiled=True)
    out = pl.pallas_call(
        unpack_kernel,
        out_shape=jax.ShapeDtypeStruct((8, GROUP), F32),
        in_specs=[VMEM] * 2,
        out_specs=VMEM,
        scratch_shapes=[pltpu.VMEM((2 * BLOCKS, 128), F32)],
        compiler_params=pltpu.CompilerParams(vmem_limit_bytes=8 << 20),
        name="unpack",
    )(ids, shared)
    return out.T


def solution(mesh):
    in_specs = (
        P(("sta", "tpl"), None, None),
        P("tpl", "sta", None, None),
        P("tpl", "sta"),
        P("tpl", "sta", None),
    )
    return jax.shard_map(
        on_device, mesh=mesh, in_specs=in_specs, out_specs=P("tpl", "sta"), check_vma=False
    )
```
